32 devices in a mesh: section: 2 (over core), tensor: 4 (over y, x), shard: 4 (over z).
Axes of the slice: x: 2, y: 2, z: 4, core: 2. Of those that a mesh axis runs over, the one named last changes fastest.
Arguments:
- attention_gradient: float32 [32, 1024, 1024], P('section', 'shard', 'tensor'), may hold values from -500 to 500, as said below
- gated_gradient: float32 [12, 1024, 2816], P('section', 'shard', 'tensor'), may hold values from -500 to 500, as said below
- attention_master: float32 [32, 256, 4, 1024], P('section', 'shard', None, 'tensor'), may hold values from -0.12 to 0.12
- gated_master: float32 [12, 256, 4, 2816], P('section', 'shard', None, 'tensor'), may hold values from -0.12 to 0.12
- attention_momentum: float32 [32, 256, 4, 1024], P('section', 'shard', None, 'tensor'), may hold values from -4 to 4
- gated_momentum: float32 [12, 256, 4, 2816], P('section', 'shard', None, 'tensor'), may hold values from -4 to 4
- attention_variance: float32 [32, 256, 4, 1024], P('section', 'shard', None, 'tensor'), may hold values from 0.005 to 0.2
- gated_variance: float32 [12, 256, 4, 2816], P('section', 'shard', None, 'tensor'), may hold values from 0.005 to 0.2
- attention_average: float32 [32, 4, 256, 1024], P(None, 'shard', 'section', 'tensor'), may hold values from -0.12 to 0.12
- gated_average: float32 [12, 4, 256, 2816], P(None, 'shard', 'section', 'tensor'), may hold values from -0.12 to 0.12
Outputs:
- master_attention: float32 [32, 256, 4, 1024], P('section', 'shard', None, 'tensor')
- master_gated: float32 [12, 256, 4, 2816], P('section', 'shard', None, 'tensor')
- momentum_attention: float32 [32, 256, 4, 1024], P('section', 'shard', None, 'tensor')
- momentum_gated: float32 [12, 256, 4, 2816], P('section', 'shard', None, 'tensor')
- variance_attention: float32 [32, 256, 4, 1024], P('section', 'shard', None, 'tensor')
- variance_gated: float32 [12, 256, 4, 2816], P('section', 'shard', None, 'tensor')
- weights_attention: bfloat16 [32, 1024, 1024], P('section', 'shard', 'tensor')
- weights_gated: bfloat16 [12, 1024, 2816], P('section', 'shard', 'tensor')
- average_attention: float32 [32, 4, 256, 1024], P(None, 'shard', 'section', 'tensor')
- average_gated: float32 [12, 4, 256, 2816], P(None, 'shard', 'section', 'tensor')
The draws below stay inside these ranges and needn't reach their ends.
Inputs may be any that keep to these rules, and one draw needn't show every extreme that they name: `attention_gradient`: gradient entries of either sign. `gated_gradient`: gradient entries of either sign.
All inputs are finite; a program needn't handle non-finite values.
Results may differ from the reference program's by a relative error of at most 0.0018.
Values may be sent and summed in bfloat16 or wider, within the bound.
No kernel may reach another device: no remote copies, remote signals or barrier semaphores. Data moves between devices by JAX's collectives and lax.ppermute only.
A program may use at most 192 MiB of HBM per device.

```python
import math
import jax
import jax.numpy as jnp

D = 1024
FF = 2816
STEP = 20
AVG_COUNT = 3
HH = 1024
K_ATT = 32
K_FF = 12
ROW_BLOCKS = 4
ROW_SUB = 256
ENTRIES = 68157440


COLUMN_REGION = 128


LEVEL_SPREAD = 1.5


def rising_scale(mat_count, row_count, col_count):
    lift = math.log(3.0)
    depth_part = jnp.arange(mat_count, dtype=jnp.float32)[:, None, None] / max(mat_count - 1, 1)
    row_part = jnp.arange(row_count, dtype=jnp.float32)[None, :, None] / max(row_count - 1, 1)
    col_part = jnp.arange(col_count, dtype=jnp.float32)[None, None, :] / max(col_count - 1, 1)
    return jnp.exp(lift * (depth_part + row_part + col_part))


def region_level(key, mat_count, col_count):
    region_count = (col_count + COLUMN_REGION - 1) // COLUMN_REGION
    exponents = jax.random.uniform(jax.random.fold_in(key, 13), (mat_count, region_count), jnp.float32, -LEVEL_SPREAD, LEVEL_SPREAD)
    column_region = jnp.arange(col_count) // COLUMN_REGION
    levels = jnp.exp(exponents)[:, column_region]
    return levels[:, None, :]


def drawn_gradient(key, mat_count, row_count, col_count):
    values = jax.random.truncated_normal(jax.random.fold_in(key, 7), -4.0, 4.0, (mat_count, row_count, col_count), jnp.float32)
    return values * rising_scale(mat_count, row_count, col_count) * region_level(key, mat_count, col_count)


def draw_attention_gradient(key, part):
    return drawn_gradient(key, K_ATT, D, HH)


def draw_gated_gradient(key, part):
    return drawn_gradient(key, K_FF, D, FF)


def steps_of(rng, dims, cuts, smallest, high):
    def one(position, parts):
        heights = jax.random.uniform(jax.random.fold_in(jax.random.fold_in(rng, 6), position), (parts,), jnp.float32, smallest / len(cuts), high / len(cuts))
        return jnp.repeat(jnp.exp(heights), dims[position] // parts).reshape((-1,) + (1,) * (len(dims) - position - 1))

    gain = one(*cuts[0])
    for cut in cuts[1:]:
        gain = gain * one(*cut)
    return gain


def centred(own_key, extent, deviation, most, shards=(), held_as=jnp.bfloat16):
    gain = steps_of(own_key, extent, shards, -0.22, 0.18) if shards else 1.0
    result = jax.random.normal(own_key, extent, jnp.float32) * deviation * gain
    return jnp.minimum(jnp.maximum(result, -most), most).astype(held_as)


def setup_inputs(seed: int = 0) -> dict:
    key_list = jax.random.split(jax.random.key(seed), 11)
    return {
        "attention_gradient": draw_attention_gradient(jax.random.fold_in(key_list[10], 71), 0),
        "gated_gradient": draw_gated_gradient(jax.random.fold_in(key_list[10], 71), 0),
        "attention_master": centred(key_list[2], (K_ATT, ROW_SUB, ROW_BLOCKS, HH), 0.02, 0.12, ((0, 2), (1, 4), (3, 4)), jnp.float32),
        "gated_master": centred(key_list[3], (K_FF, ROW_SUB, ROW_BLOCKS, FF), 0.02, 0.12, ((0, 2), (1, 4), (3, 4)), jnp.float32),
        "attention_momentum": centred(key_list[4], (K_ATT, ROW_SUB, ROW_BLOCKS, HH), 0.3, 4.0, ((0, 2), (1, 4), (3, 4)), jnp.float32),
        "gated_momentum": centred(key_list[5], (K_FF, ROW_SUB, ROW_BLOCKS, FF), 0.3, 4.0, ((0, 2), (1, 4), (3, 4)), jnp.float32),
        "attention_variance": jnp.clip(jnp.exp(math.log(0.2) - 3.6888795 * jax.random.uniform(key_list[6], (K_ATT, ROW_SUB, ROW_BLOCKS, HH), jnp.float32) ** steps_of(key_list[6], (K_ATT, ROW_SUB, ROW_BLOCKS, HH), ((0, 2), (1, 4), (3, 4)), -0.2, 0.2)), 0.005, 0.2),
        "gated_variance": jnp.clip(jnp.exp(math.log(0.2) - 3.6888795 * jax.random.uniform(key_list[7], (K_FF, ROW_SUB, ROW_BLOCKS, FF), jnp.float32) ** steps_of(key_list[7], (K_FF, ROW_SUB, ROW_BLOCKS, FF), ((0, 2), (1, 4), (3, 4)), -0.2, 0.2)), 0.005, 0.2),
        "attention_average": centred(key_list[8], (K_ATT, ROW_BLOCKS, ROW_SUB, HH), 0.02, 0.12, ((1, 4), (2, 2), (3, 4)), jnp.float32),
        "gated_average": centred(key_list[9], (K_FF, ROW_BLOCKS, ROW_SUB, FF), 0.02, 0.12, ((1, 4), (2, 2), (3, 4)), jnp.float32),
    }


BETA_FIRST = 0.9
BETA_SECOND = 0.95
ADAM_EPSILON = 1e-08
LEARN_RATE = 0.001
DECAY_RATE = 0.1
CLIP_LEVEL = 0.5

def adamw_update(gradient, master, momentum, variance, factor):
    clipped = gradient * factor
    momentum_new = BETA_FIRST * momentum + (1.0 - BETA_FIRST) * clipped
    variance_new = BETA_SECOND * variance + (1.0 - BETA_SECOND) * clipped * clipped
    first_fix = 1.0 - BETA_FIRST ** STEP
    second_fix = 1.0 - BETA_SECOND ** STEP
    direction = momentum_new / first_fix / (jnp.sqrt(variance_new / second_fix) + ADAM_EPSILON)
    master_new = master - LEARN_RATE * (direction + DECAY_RATE * master)
    return (master_new, momentum_new, variance_new)

def to_pieces(blocks_array):
    return blocks_array.reshape(blocks_array.shape[0], ROW_BLOCKS, ROW_SUB, blocks_array.shape[2]).transpose(0, 2, 1, 3)

def from_pieces(pieces_array):
    return pieces_array.transpose(0, 2, 1, 3).reshape(pieces_array.shape[0], D, pieces_array.shape[3])

def reference(attention_gradient, gated_gradient, attention_master, gated_master, attention_momentum, gated_momentum, attention_variance, gated_variance, attention_average, gated_average):
    squares = jnp.sum(attention_gradient * attention_gradient) + jnp.sum(gated_gradient * gated_gradient)
    factor = jnp.minimum(1.0, CLIP_LEVEL * math.sqrt(ENTRIES) / jnp.sqrt(squares))
    groups = ((attention_gradient, attention_master, attention_momentum, attention_variance, attention_average), (gated_gradient, gated_master, gated_momentum, gated_variance, gated_average))
    masters = []
    moments = []
    variances = []
    weights = []
    averages = []
    for gradient, master, momentum, variance, average in groups:
        master_new, momentum_new, variance_new = adamw_update(to_pieces(gradient), master, momentum, variance, factor)
        blocked = from_pieces(master_new)
        masters.append(master_new)
        moments.append(momentum_new)
        variances.append(variance_new)
        weights.append(blocked.astype(jnp.bfloat16))
        averages.append(average + (blocked.reshape(average.shape) - average) / (AVG_COUNT + 1.0))
    return (masters[0], masters[1], moments[0], moments[1], variances[0], variances[1], weights[0], weights[1], averages[0], averages[1])
```

```python
import math

import jax
import jax.numpy as jnp
from jax import lax
from jax.sharding import PartitionSpec as P

STEP = 20
AVG_COUNT = 3
ENTRIES = 68157440


BETA_FIRST = 0.9
BETA_SECOND = 0.95
ADAM_EPSILON = 1e-08
LEARN_RATE = 0.001
DECAY_RATE = 0.1
CLIP_LEVEL = 0.5

LIFT = 2.0**22


def encode(gradient):
    lifted = gradient * LIFT
    squared = lifted * jnp.abs(lifted)
    return (squared * jnp.abs(squared)).astype(jnp.bfloat16)


def decode(code):
    wide = code.astype(jnp.float32)
    root = lax.rsqrt(lax.rsqrt(jnp.abs(wide)))
    return jnp.where(wide < 0, -root, root) * (1.0 / LIFT)


def adamw_update(gradient, master, momentum, variance, factor):
    clipped = gradient * factor
    momentum_new = BETA_FIRST * momentum + (1.0 - BETA_FIRST) * clipped
    variance_new = BETA_SECOND * variance + (1.0 - BETA_SECOND) * clipped * clipped
    first_fix = 1.0 - BETA_FIRST**STEP
    second_fix = 1.0 - BETA_SECOND**STEP
    direction = momentum_new / first_fix / (jnp.sqrt(variance_new / second_fix) + ADAM_EPSILON)
    master_new = master - LEARN_RATE * (direction + DECAY_RATE * master)
    return (master_new, momentum_new, variance_new)


def average_update(average, rows_master):
    return average + (rows_master - average) / (AVG_COUNT + 1.0)


def total(value, axis):
    count = lax.axis_size(axis)
    if count & (count - 1):
        return lax.psum(value, axis)
    step = 1
    while step < count:
        value = value + lax.ppermute(value, axis, [(i, i ^ step) for i in range(count)])
        step *= 2
    return value


def send_gradient(gradient, shard_count):
    mats, rows, cols = gradient.shape
    code = encode(gradient).reshape(mats, shard_count, rows // shard_count, cols)
    return lax.all_to_all(code.transpose(1, 0, 2, 3), "shard", split_axis=0, concat_axis=0, tiled=True)


def send_weights(master):
    narrow = master.astype(jnp.bfloat16).transpose(2, 0, 1, 3)
    blocks = lax.all_to_all(narrow, "shard", split_axis=0, concat_axis=0, tiled=True)
    return blocks.transpose(1, 0, 2, 3).reshape(
        blocks.shape[1], blocks.shape[0] * blocks.shape[2], blocks.shape[3]
    )


def send_halves(weights):
    mats, rows, cols = weights.shape
    count = lax.axis_size("section")
    halves = weights.reshape(mats, count, rows // count, cols)
    halves = lax.all_to_all(halves, "section", split_axis=1, concat_axis=0, tiled=True)
    return halves.astype(jnp.float32)


def shards(
    attention_gradient,
    gated_gradient,
    attention_master,
    gated_master,
    attention_momentum,
    gated_momentum,
    attention_variance,
    gated_variance,
    attention_average,
    gated_average,
):
    shard_count = lax.axis_size("shard")
    gated_piece = send_gradient(gated_gradient, shard_count)
    squares = jnp.sum(attention_gradient * attention_gradient) + jnp.sum(gated_gradient * gated_gradient)
    squares = jnp.full((8, 128), squares)
    for axis in ("section", "tensor"):
        squares = total(squares, axis)
    squares, gated_piece = lax.optimization_barrier((squares, gated_piece))
    squares = total(squares, "shard")
    squares, attention_gradient = lax.optimization_barrier((squares, attention_gradient))
    squares = squares[0, 0]
    attention_piece = send_gradient(attention_gradient, shard_count)
    factor = jnp.minimum(1.0, CLIP_LEVEL * math.sqrt(ENTRIES) / jnp.sqrt(squares))
    gated_new, gated_moment, gated_spread = adamw_update(
        decode(gated_piece).transpose(1, 2, 0, 3), gated_master, gated_momentum, gated_variance, factor
    )
    attention_new, attention_moment, attention_spread = adamw_update(
        decode(attention_piece).transpose(1, 2, 0, 3), attention_master, attention_momentum, attention_variance, factor
    )
    gated_weights = send_weights(gated_new)
    attention_weights = send_weights(attention_new)
    gated_averaged = average_update(gated_average, send_halves(gated_weights))
    attention_averaged = average_update(attention_average, send_halves(attention_weights))
    return (
        attention_new,
        gated_new,
        attention_moment,
        gated_moment,
        attention_spread,
        gated_spread,
        attention_weights,
        gated_weights,
        attention_averaged,
        gated_averaged,
    )


STATE = P("section", "shard", None, "tensor")
BLOCK = P("section", "shard", "tensor")
ROWS = P(None, "shard", "section", "tensor")


def solution(mesh):
    return jax.shard_map(
        shards,
        mesh=mesh,
        in_specs=(BLOCK,) * 2 + (STATE,) * 6 + (ROWS,) * 2,
        out_specs=(STATE,) * 6 + (BLOCK,) * 2 + (ROWS,) * 2,
        check_vma=False,
    )
```

```python
import math

import jax
import jax.numpy as jnp
from jax import lax
from jax.experimental import pallas as pl
from jax.experimental.pallas import tpu as pltpu
from jax.sharding import PartitionSpec as P

STEP = 20
AVG_COUNT = 3
ENTRIES = 68157440


BETA_FIRST = 0.9
BETA_SECOND = 0.95
ADAM_EPSILON = 1e-08
LEARN_RATE = 0.001
DECAY_RATE = 0.1
CLIP_LEVEL = 0.5

LIFT = 2.0**22


def encode_wide(gradient):
    lifted = gradient * LIFT
    squared = lifted * jnp.abs(lifted)
    return squared * jnp.abs(squared)


def encode(gradient):
    return encode_wide(gradient).astype(jnp.bfloat16)


def decode(code):
    wide = code.astype(jnp.float32)
    root = lax.rsqrt(lax.rsqrt(jnp.abs(wide)))
    return jnp.where(wide < 0, -root, root) * (1.0 / LIFT)


def adamw_update(gradient, master, momentum, variance, factor):
    clipped = gradient * factor
    momentum_new = BETA_FIRST * momentum + (1.0 - BETA_FIRST) * clipped
    variance_new = BETA_SECOND * variance + (1.0 - BETA_SECOND) * clipped * clipped
    first_fix = 1.0 - BETA_FIRST**STEP
    second_fix = 1.0 - BETA_SECOND**STEP
    direction = momentum_new / first_fix / (jnp.sqrt(variance_new / second_fix) + ADAM_EPSILON)
    master_new = master - LEARN_RATE * (direction + DECAY_RATE * master)
    return (master_new, momentum_new, variance_new)


def average_update(average, rows_master):
    return average + (rows_master - average) / (AVG_COUNT + 1.0)


def total(value, axis):
    count = lax.axis_size(axis)
    if count & (count - 1):
        return lax.psum(value, axis)
    step = 1
    while step < count:
        value = value + lax.ppermute(value, axis, [(i, i ^ step) for i in range(count)])
        step *= 2
    return value


def send_gradient(gradient, shard_count):
    mats, rows, cols = gradient.shape
    code = encode(gradient).reshape(mats, shard_count, rows // shard_count, cols)
    return lax.all_to_all(code.transpose(1, 0, 2, 3), "shard", split_axis=0, concat_axis=0, tiled=True)


def send_weights(master):
    narrow = master.astype(jnp.bfloat16).transpose(2, 0, 1, 3)
    blocks = lax.all_to_all(narrow, "shard", split_axis=0, concat_axis=0, tiled=True)
    return blocks.transpose(1, 0, 2, 3).reshape(
        blocks.shape[1], blocks.shape[0] * blocks.shape[2], blocks.shape[3]
    )


def send_halves(weights):
    mats, rows, cols = weights.shape
    count = lax.axis_size("section")
    halves = weights.reshape(mats, count, rows // count, cols)
    halves = lax.all_to_all(halves, "section", split_axis=1, concat_axis=0, tiled=True)
    return halves.astype(jnp.float32)


def plain_shards(
    attention_gradient,
    gated_gradient,
    attention_master,
    gated_master,
    attention_momentum,
    gated_momentum,
    attention_variance,
    gated_variance,
    attention_average,
    gated_average,
):
    shard_count = lax.axis_size("shard")
    gated_piece = send_gradient(gated_gradient, shard_count)
    squares = jnp.sum(attention_gradient * attention_gradient) + jnp.sum(gated_gradient * gated_gradient)
    squares = jnp.full((8, 128), squares)
    for axis in ("section", "tensor"):
        squares = total(squares, axis)
    squares, gated_piece = lax.optimization_barrier((squares, gated_piece))
    squares = total(squares, "shard")
    squares, attention_gradient = lax.optimization_barrier((squares, attention_gradient))
    squares = squares[0, 0]
    attention_piece = send_gradient(attention_gradient, shard_count)
    factor = jnp.minimum(1.0, CLIP_LEVEL * math.sqrt(ENTRIES) / jnp.sqrt(squares))
    gated_new, gated_moment, gated_spread = adamw_update(
        decode(gated_piece).transpose(1, 2, 0, 3), gated_master, gated_momentum, gated_variance, factor
    )
    attention_new, attention_moment, attention_spread = adamw_update(
        decode(attention_piece).transpose(1, 2, 0, 3), attention_master, attention_momentum, attention_variance, factor
    )
    gated_weights = send_weights(gated_new)
    attention_weights = send_weights(attention_new)
    gated_averaged = average_update(gated_average, send_halves(gated_weights))
    attention_averaged = average_update(attention_average, send_halves(attention_weights))
    return (
        attention_new,
        gated_new,
        attention_moment,
        gated_moment,
        attention_spread,
        gated_spread,
        attention_weights,
        gated_weights,
        attention_averaged,
        gated_averaged,
    )


LANES = 128
HALF = LANES // 2


def by_owner(values, me):
    odd = (me & 1) == 1
    high = (me & 2) == 2
    values = [jnp.where(odd, values[j ^ 1], values[j]) for j in range(4)]
    return [jnp.where(high, values[j ^ 2], values[j]) for j in range(4)]


def fold_sum(block):
    return jnp.sum(block.reshape(-1, 8, LANES), axis=0)


def swap_halves(block):
    return pltpu.roll(block, HALF, 1)


def left_lanes(block):
    return lax.broadcasted_iota(jnp.int32, block.shape, 1) < HALF


def attention_encode_kernel(place, *refs):
    inputs, outputs, sum_ref = refs[:4], refs[4:7], refs[7]

    @pl.when(pl.program_id(0) == 0)
    def _():
        sum_ref[...] = jnp.zeros_like(sum_ref)

    total_squares = sum_ref[...]
    for j in range(4):
        for k in range(inputs[j].shape[0]):
            block = inputs[j][k]
            squared = block * block
            for tile in range(block.shape[1] // LANES):
                total_squares += fold_sum(squared[:, tile * LANES : (tile + 1) * LANES])
            if j:
                outputs[j - 1][k] = encode(block)
    sum_ref[...] = total_squares


def attention_encode(place, gradient, first, count, step):
    mats, rows, cols = gradient.shape
    piece = rows // 4

    def taken(j):
        return pl.BlockSpec((step, piece, cols), lambda i, p: (first // step + i, p[0] ^ j, 0))

    given = pl.BlockSpec((step, piece, cols), lambda i, p: (i, 0, 0))
    return pl.pallas_call(
        attention_encode_kernel,
        grid_spec=pltpu.PrefetchScalarGridSpec(
            num_scalar_prefetch=1,
            grid=(count // step,),
            in_specs=[taken(j) for j in range(4)],
            out_specs=[given] * 3 + [pl.BlockSpec((8, LANES), lambda i, p: (0, 0))],
        ),
        out_shape=[jax.ShapeDtypeStruct((count, piece, cols), jnp.bfloat16)] * 3
        + [jax.ShapeDtypeStruct((8, LANES), jnp.float32)],
        name="attention_encode",
    )(place, *[gradient] * 4)


def gated_encode_kernel(place, grad_ref, out0, out1, out2, out3, sum_ref, turned):
    me = place[0]

    @pl.when(pl.program_id(0) == 0)
    def _():
        sum_ref[...] = jnp.zeros_like(sum_ref)

    cols, rows = grad_ref.shape[1:]
    block = grad_ref[0]
    squared = block * block
    total_squares = sum_ref[...]
    for tile in range(rows // LANES):
        total_squares += fold_sum(squared[:, tile * LANES : (tile + 1) * LANES])
    sum_ref[...] = total_squares
    code = encode_wide(block)
    turned[:, :cols] = code.T
    piece = rows // 4
    full = cols // LANES
    for j, out in enumerate((out0, out1, out2, out3)):
        start = pl.multiple_of((me ^ j) * piece, piece)
        for tile in range(full):
            lanes = slice(tile * LANES, (tile + 1) * LANES)
            out[0, tile * piece : (tile + 1) * piece, :] = turned[pl.ds(start, piece), lanes].astype(jnp.bfloat16)
        last = turned[pl.ds(start, piece), full * LANES : (full + 1) * LANES]
        upper, lower = last[: piece // 2], last[piece // 2 :]
        out[0, full * piece :, :] = jnp.where(left_lanes(upper), upper, swap_halves(lower)).astype(jnp.bfloat16)


def gated_encode(place, turned_gradient):
    mats, cols, rows = turned_gradient.shape
    packed = rows // 4 * cols // LANES
    given = pl.BlockSpec((1, packed, LANES), lambda i, p: (i, 0, 0))
    return pl.pallas_call(
        gated_encode_kernel,
        grid_spec=pltpu.PrefetchScalarGridSpec(
            num_scalar_prefetch=1,
            grid=(mats,),
            in_specs=[pl.BlockSpec((1, cols, rows), lambda i, p: (i, 0, 0))],
            out_specs=[given] * 4 + [pl.BlockSpec((8, LANES), lambda i, p: (0, 0))],
            scratch_shapes=[pltpu.VMEM((rows, (cols // LANES + 1) * LANES), jnp.float32)],
        ),
        out_shape=[jax.ShapeDtypeStruct((mats, packed, LANES), jnp.bfloat16)] * 4
        + [jax.ShapeDtypeStruct((8, LANES), jnp.float32)],
        name="gated_encode",
    )(place, turned_gradient)


def update_rows(grads, me, factor, rows, lanes, states, news):
    masters = []
    for a, grad in enumerate(by_owner(grads, me)):
        new = adamw_update(grad, *[ref[0, rows, a, lanes] for ref in states], factor)
        for ref, value in zip(news, new):
            ref[0, rows, a, lanes] = value
        masters.append(new[0])
    return masters


def attention_step_kernel(place, factor_ref, own, in1, in2, in3, *refs):
    me, factor = place[0], factor_ref[0, 0]
    states, news, outs = refs[:3], refs[-7:-4], refs[-4:]
    for start in range(0, own.shape[1], 16):
        rows = pl.ds(start, 16)
        for tile in range(own.shape[2] // LANES):
            lanes = pl.ds(tile * LANES, LANES)
            grads = [own[0, rows, lanes]] + [decode(ref[0, rows, lanes]) for ref in (in1, in2, in3)]
            masters = update_rows(grads, me, factor, rows, lanes, states, news)
            for out, new in zip(outs, by_owner(masters, me)):
                out[0, rows, lanes] = new.astype(jnp.bfloat16)


def attention_step(place, factor, gradient, received, states, before, first, count):
    _, piece, cols = received[0].shape
    state = pl.BlockSpec((1, piece, 4, cols), lambda i, p: (first + i, 0, 0, 0))
    block = pl.BlockSpec((1, piece, cols), lambda i, p: (i, 0, 0))
    taken = pl.BlockSpec((1, piece, cols), lambda i, p: (first + i, 0, 0))
    own = pl.BlockSpec((1, piece, cols), lambda i, p: (first + i, p[0], 0))
    whole = pl.BlockSpec(memory_space=pl.ANY)
    return pl.pallas_call(
        attention_step_kernel,
        grid_spec=pltpu.PrefetchScalarGridSpec(
            num_scalar_prefetch=1,
            grid=(count,),
            in_specs=[pl.BlockSpec(memory_space=pltpu.SMEM), own] + [taken] * 3 + [state] * 3 + [whole] * len(before),
            out_specs=[state] * 3 + [block] * 4,
        ),
        out_shape=[jax.ShapeDtypeStruct(states[0].shape, jnp.float32)] * 3
        + [jax.ShapeDtypeStruct((count, piece, cols), jnp.bfloat16)] * 4,
        input_output_aliases={9 + i: i for i in range(len(before))},
        name="attention_step",
    )(place, factor, gradient, *received, *states, *before)


def gated_step_kernel(place, factor_ref, in0, in1, in2, in3, *refs):
    me, factor = place[0], factor_ref[0, 0]
    states, news, out, narrow = refs[:3], refs[3:6], refs[6], refs[7]
    ins = (in0, in1, in2, in3)
    piece, cols = states[0].shape[1], states[0].shape[3]
    full, half = cols // LANES, piece // 2
    for tile in range(full):
        lanes = pl.ds(tile * LANES, LANES)
        for start in range(0, piece, 16):
            rows = pl.ds(start, 16)
            grads = [decode(ref[0, pl.ds(tile * piece + start, 16), :]) for ref in ins]
            for a, new in enumerate(update_rows(grads, me, factor, rows, lanes, states, news)):
                narrow[a // 2, pl.ds(a % 2 * piece + start, 16), lanes] = new
    lanes = pl.ds(full * LANES, HALF)
    for start in range(0, half, 16):
        both = [decode(ref[0, pl.ds(full * piece + start, 16), :]) for ref in ins]
        for side in range(2):
            rows = pl.ds(side * half + start, 16)
            grads = [(swap_halves(grad) if side else grad)[:, :HALF] for grad in both]
            for a, new in enumerate(update_rows(grads, me, factor, rows, lanes, states, news)):
                narrow[a // 2, pl.ds(a % 2 * piece + side * half + start, 16), lanes] = new
    middle = cols // 2
    for pair in range(2):
        turned = narrow[pair].T
        top, bottom = turned[:middle], turned[middle:cols]
        left = left_lanes(top)
        out[2 * pair, 0] = jnp.where(left, top, swap_halves(bottom)).astype(jnp.bfloat16)
        out[2 * pair + 1, 0] = jnp.where(left, swap_halves(top), bottom).astype(jnp.bfloat16)


def gated_step(place, factor, received, states):
    count, packed, _ = received[0].shape
    piece, cols = states[0].shape[1], states[0].shape[3]
    state = pl.BlockSpec((1, piece, 4, cols), lambda i, p: (i, 0, 0, 0))
    block = pl.BlockSpec((1, packed, LANES), lambda i, p: (i, 0, 0))
    return pl.pallas_call(
        gated_step_kernel,
        grid_spec=pltpu.PrefetchScalarGridSpec(
            num_scalar_prefetch=1,
            grid=(count,),
            in_specs=[pl.BlockSpec(memory_space=pltpu.SMEM)] + [block] * 4 + [state] * 3,
            out_specs=[state] * 3 + [pl.BlockSpec((4, 1, packed, LANES), lambda i, p: (0, i, 0, 0))],
            scratch_shapes=[pltpu.VMEM((2, LANES, (cols // LANES + 1) * LANES), jnp.float32)],
        ),
        out_shape=[jax.ShapeDtypeStruct(states[0].shape, jnp.float32)] * 3
        + [jax.ShapeDtypeStruct((4, count, packed, LANES), jnp.bfloat16)],
        name="gated_step",
    )(place, factor, *received, *states)


def attention_place_kernel(place, in0, in1, in2, in3, *refs):
    me, section = place[0], place[1]
    weights, kept, sent = refs[-3:]
    piece = in0.shape[1]
    for j, ref in enumerate((in0, in1, in2, in3)):
        weights[:, pl.ds(pl.multiple_of((me ^ j) * piece, piece), piece), :] = ref[...]
    half = 2 * piece
    kept[...] = weights[:, pl.ds(pl.multiple_of(section * half, half), half), :]
    sent[...] = weights[:, pl.ds(pl.multiple_of((1 - section) * half, half), half), :]


def attention_place(place, received, before, first, count, step):
    mats, piece, cols = received[0].shape
    block = pl.BlockSpec((step, piece, cols), lambda i, p: (first // step + i, 0, 0))
    half = pl.BlockSpec((step, 2 * piece, cols), lambda i, p: (i, 0, 0))
    return pl.pallas_call(
        attention_place_kernel,
        grid_spec=pltpu.PrefetchScalarGridSpec(
            num_scalar_prefetch=1,
            grid=(count // step,),
            in_specs=[block] * 4 + [pl.BlockSpec(memory_space=pl.ANY)] * len(before),
            out_specs=[pl.BlockSpec((step, 4 * piece, cols), lambda i, p: (first // step + i, 0, 0)), half, half],
        ),
        out_shape=[jax.ShapeDtypeStruct((mats, 4 * piece, cols), jnp.bfloat16)]
        + [jax.ShapeDtypeStruct((count, 2 * piece, cols), jnp.bfloat16)] * 2,
        input_output_aliases={5 + i: i for i in range(len(before))},
        name="attention_place",
    )(place, *received, *before)


def gated_place_kernel(place, received, average, weights, sent, averaged):
    section = place[1]
    blocks = [received[d, 0].astype(jnp.float32) for d in range(4)]
    middle = received.shape[2]
    left = left_lanes(blocks[0])
    for tile in range(2):
        lanes = slice(tile * LANES, (tile + 1) * LANES)
        one, two = blocks[2 * tile : 2 * tile + 2]
        weights[0, :middle, lanes] = jnp.where(left, one, swap_halves(two)).astype(jnp.bfloat16)
        weights[0, middle:, lanes] = jnp.where(left, swap_halves(one), two).astype(jnp.bfloat16)
    first, second = weights[0, :, :LANES], weights[0, :, LANES:]

    @pl.when(section == 0)
    def _():
        averaged[0, 0] = average_update(average[0, 0], first.astype(jnp.float32))
        sent[0] = second

    @pl.when(section != 0)
    def _():
        averaged[0, 0] = average_update(average[0, 0], second.astype(jnp.float32))
        sent[0] = first


def gated_place(place, received, average):
    _, count, packed, _ = received.shape
    block = pl.BlockSpec((4, 1, packed, LANES), lambda i, p: (0, i, 0, 0))
    half = pl.BlockSpec((1, 2 * packed, LANES), lambda i, p: (i, 0, 0))
    ours = pl.BlockSpec((1, 1, 2 * packed, LANES), lambda i, p: (p[1], i, 0, 0))
    return pl.pallas_call(
        gated_place_kernel,
        grid_spec=pltpu.PrefetchScalarGridSpec(
            num_scalar_prefetch=1,
            grid=(count,),
            in_specs=[block, ours],
            out_specs=[pl.BlockSpec((1, 2 * packed, 2 * LANES), lambda i, p: (i, 0, 0)), half, ours],
        ),
        out_shape=[jax.ShapeDtypeStruct((count, 2 * packed, 2 * LANES), jnp.bfloat16)]
        + [jax.ShapeDtypeStruct((count, 2 * packed, LANES), jnp.bfloat16)]
        + [jax.ShapeDtypeStruct(average.shape, jnp.float32)],
        name="gated_place",
    )(place, received, average)


def average_kernel(place, kept, other, average, *refs):
    section = place[1]
    out = refs[-1]
    out[section] = average_update(average[section], kept[...].astype(jnp.float32))
    out[1 - section] = average_update(average[1 - section], other[...].astype(jnp.float32))


def average_rows(place, kept, other, average, before, first, step):
    count, rows, cols = kept.shape
    block = pl.BlockSpec((step, rows, cols), lambda i, p: (i, 0, 0))
    both = pl.BlockSpec((2, step, rows, cols), lambda i, p: (0, first // step + i, 0, 0))
    return pl.pallas_call(
        average_kernel,
        grid_spec=pltpu.PrefetchScalarGridSpec(
            num_scalar_prefetch=1,
            grid=(count // step,),
            in_specs=[block] * 2 + [both] + [pl.BlockSpec(memory_space=pl.ANY)] * len(before),
            out_specs=[both],
        ),
        out_shape=[jax.ShapeDtypeStruct(average.shape, jnp.float32)],
        input_output_aliases={4 + i: i for i in range(len(before))},
        name="average_rows",
    )(place, kept, other, average, *before)


def average_others_kernel(place, other, average, before, out):
    out[0] = average_update(average[0], other[...].astype(jnp.float32))


def average_others(place, other, average, before):
    count, rows, cols = other.shape
    theirs = pl.BlockSpec((1, 1, rows, cols), lambda i, p: (1 - p[1], i, 0, 0))
    return pl.pallas_call(
        average_others_kernel,
        grid_spec=pltpu.PrefetchScalarGridSpec(
            num_scalar_prefetch=1,
            grid=(count,),
            in_specs=[pl.BlockSpec((1, rows, cols), lambda i, p: (i, 0, 0)), theirs, pl.BlockSpec(memory_space=pl.ANY)],
            out_specs=theirs,
        ),
        out_shape=jax.ShapeDtypeStruct(average.shape, jnp.float32),
        input_output_aliases={3: 0},
        name="average_others",
    )(place, other, average, before)


def shards_swap(parts):
    return lax.all_to_all(parts, "shard", split_axis=0, concat_axis=0, tiled=True)


def swap_far_first(values):
    moved = {}
    for j in (3, 2, 1):
        moved[j] = lax.ppermute(values[j - 1], "shard", [(i, i ^ j) for i in range(4)])
    return [moved[j] for j in (1, 2, 3)]


def after(value, done):
    return lax.optimization_barrier((value, done))


def cores(half):
    return lax.ppermute(half, "section", [(0, 1), (1, 0)])


def tuned_shards(
    attention_gradient,
    gated_gradient,
    attention_master,
    gated_master,
    attention_momentum,
    gated_momentum,
    attention_variance,
    gated_variance,
    attention_average,
    gated_average,
):
    place = jnp.stack([lax.axis_index("shard"), lax.axis_index("section")]).astype(jnp.int32)
    mats = attention_gradient.shape[0]
    attention_states = (attention_master, attention_momentum, attention_variance)
    gated_states = (gated_master, gated_momentum, gated_variance)

    *gated_code, gated_squares = gated_encode(place, gated_gradient.swapaxes(1, 2))
    gated_in = gated_code[:1] + swap_far_first(gated_code[1:])
    later_gradient, gated_squares = after(attention_gradient, gated_squares)
    *code, squares = attention_encode(place, later_gradient, 0, mats, 4)
    squares = jnp.sum(gated_squares + squares)
    squares = lax.psum(squares, ("section", "tensor"))
    gated_in, squares = after(gated_in, squares)
    squares = shards_swap(jnp.full((4, 8, LANES), squares))
    code, squares = after(code, squares)
    squares = jnp.sum(squares, axis=0)
    attention_in = swap_far_first(code)
    factor = jnp.minimum(1.0, CLIP_LEVEL * math.sqrt(ENTRIES) / jnp.sqrt(squares[:1, :1]))

    *gated_new, narrow = gated_step(place, factor, gated_in, gated_states)
    narrow, attention_in = after(narrow, attention_in)
    gated_out = shards_swap(narrow)
    *attention_new, own, one, two, three = attention_step(
        place, factor, attention_gradient, attention_in, attention_states, (), 0, mats
    )
    attention_out = [own] + swap_far_first([one, two, three])

    gated_rows = gated_average.swapaxes(2, 3)
    gated_shape = gated_rows.shape
    gated_rows = gated_rows.reshape(2, -1, *gated_shape[2:])
    gated_out, own = after(gated_out, own)
    gated_weights, sent, gated_averaged = gated_place(place, gated_out, gated_rows)
    attention_out, sent = after(attention_out, sent)
    gated_other = cores(sent)

    rows, cols = attention_average.shape[2:]
    attention_rows = attention_average.reshape(2, mats, rows, cols)
    half = mats // 2
    weights, first_kept, sent = attention_place(place, attention_out, (), 0, half, 4)
    first_other = cores(sent)
    attention_weights, last_kept, sent = attention_place(place, attention_out, (weights,), half, half, 4)
    last_other = cores(sent)
    averaged = average_rows(place, first_kept, first_other, attention_rows, (), 0, 4)
    (averaged,) = average_rows(place, last_kept, last_other, attention_rows, averaged, half, 4)
    gated_other, averaged = after(gated_other, averaged)
    gated_averaged = average_others(place, gated_other, gated_rows, gated_averaged)
    gated_averaged = gated_averaged.reshape(gated_shape).swapaxes(2, 3)
    return (
        attention_new[0],
        gated_new[0],
        attention_new[1],
        gated_new[1],
        attention_new[2],
        gated_new[2],
        attention_weights,
        gated_weights.swapaxes(1, 2),
        averaged.reshape(attention_average.shape),
        gated_averaged,
    )


def fits(attention_gradient, gated_gradient, gated_master):
    mats, rows, cols = attention_gradient.shape
    return (
        lax.axis_size("shard") == 4
        and lax.axis_size("section") == 2
        and rows == 2 * LANES
        and cols % LANES == 0
        and mats % 8 == 0
        and gated_gradient.shape[0] % 2 == 0
        and gated_gradient.shape[1] == rows
        and gated_gradient.shape[2] % LANES == HALF
        and gated_master.shape[1:3] == (HALF, 4)
    )


def shards(*arrays):
    if fits(arrays[0], arrays[1], arrays[3]):
        return tuned_shards(*arrays)
    return plain_shards(*arrays)


STATE = P("section", "shard", None, "tensor")
BLOCK = P("section", "shard", "tensor")
ROWS = P(None, "shard", "section", "tensor")


def solution(mesh):
    return jax.shard_map(
        shards,
        mesh=mesh,
        in_specs=(BLOCK,) * 2 + (STATE,) * 6 + (ROWS,) * 2,
        out_specs=(STATE,) * 6 + (BLOCK,) * 2 + (ROWS,) * 2,
        check_vma=False,
    )
```

```python
import math

import jax
import jax.numpy as jnp
from jax import lax
from jax.experimental import pallas as pl
from jax.experimental.pallas import tpu as pltpu
from jax.sharding import PartitionSpec as P

STEP = 20
AVG_COUNT = 3
ENTRIES = 68157440


BETA_FIRST = 0.9
BETA_SECOND = 0.95
ADAM_EPSILON = 1e-08
LEARN_RATE = 0.001
DECAY_RATE = 0.1
CLIP_LEVEL = 0.5

LIFT = 2.0**22


def encode_wide(gradient):
    lifted = gradient * LIFT
    squared = lifted * jnp.abs(lifted)
    return squared * jnp.abs(squared)


def encode(gradient):
    return encode_wide(gradient).astype(jnp.bfloat16)


def decode(code):
    wide = code.astype(jnp.float32)
    root = lax.rsqrt(lax.rsqrt(jnp.abs(wide)))
    return jnp.where(wide < 0, -root, root) * (1.0 / LIFT)


def adamw_update(gradient, master, momentum, variance, factor):
    clipped = gradient * factor
    momentum_new = BETA_FIRST * momentum + (1.0 - BETA_FIRST) * clipped
    variance_new = BETA_SECOND * variance + (1.0 - BETA_SECOND) * clipped * clipped
    first_fix = 1.0 - BETA_FIRST**STEP
    second_fix = 1.0 - BETA_SECOND**STEP
    direction = momentum_new / first_fix / (jnp.sqrt(variance_new / second_fix) + ADAM_EPSILON)
    master_new = master - LEARN_RATE * (direction + DECAY_RATE * master)
    return (master_new, momentum_new, variance_new)


def average_update(average, rows_master):
    return average + (rows_master - average) / (AVG_COUNT + 1.0)


def total(value, axis):
    count = lax.axis_size(axis)
    if count & (count - 1):
        return lax.psum(value, axis)
    step = 1
    while step < count:
        value = value + lax.ppermute(value, axis, [(i, i ^ step) for i in range(count)])
        step *= 2
    return value


def send_gradient(gradient, shard_count):
    mats, rows, cols = gradient.shape
    code = encode(gradient).reshape(mats, shard_count, rows // shard_count, cols)
    return lax.all_to_all(code.transpose(1, 0, 2, 3), "shard", split_axis=0, concat_axis=0, tiled=True)


def send_weights(master):
    narrow = master.astype(jnp.bfloat16).transpose(2, 0, 1, 3)
    blocks = lax.all_to_all(narrow, "shard", split_axis=0, concat_axis=0, tiled=True)
    return blocks.transpose(1, 0, 2, 3).reshape(
        blocks.shape[1], blocks.shape[0] * blocks.shape[2], blocks.shape[3]
    )


def send_halves(weights):
    mats, rows, cols = weights.shape
    count = lax.axis_size("section")
    halves = weights.reshape(mats, count, rows // count, cols)
    halves = lax.all_to_all(halves, "section", split_axis=1, concat_axis=0, tiled=True)
    return halves.astype(jnp.float32)


def plain_shards(
    attention_gradient,
    gated_gradient,
    attention_master,
    gated_master,
    attention_momentum,
    gated_momentum,
    attention_variance,
    gated_variance,
    attention_average,
    gated_average,
):
    shard_count = lax.axis_size("shard")
    gated_piece = send_gradient(gated_gradient, shard_count)
    squares = jnp.sum(attention_gradient * attention_gradient) + jnp.sum(gated_gradient * gated_gradient)
    squares = jnp.full((8, 128), squares)
    for axis in ("section", "tensor"):
        squares = total(squares, axis)
    squares, gated_piece = lax.optimization_barrier((squares, gated_piece))
    squares = total(squares, "shard")
    squares, attention_gradient = lax.optimization_barrier((squares, attention_gradient))
    squares = squares[0, 0]
    attention_piece = send_gradient(attention_gradient, shard_count)
    factor = jnp.minimum(1.0, CLIP_LEVEL * math.sqrt(ENTRIES) / jnp.sqrt(squares))
    gated_new, gated_moment, gated_spread = adamw_update(
        decode(gated_piece).transpose(1, 2, 0, 3), gated_master, gated_momentum, gated_variance, factor
    )
    attention_new, attention_moment, attention_spread = adamw_update(
        decode(attention_piece).transpose(1, 2, 0, 3), attention_master, attention_momentum, attention_variance, factor
    )
    gated_weights = send_weights(gated_new)
    attention_weights = send_weights(attention_new)
    gated_averaged = average_update(gated_average, send_halves(gated_weights))
    attention_averaged = average_update(attention_average, send_halves(attention_weights))
    return (
        attention_new,
        gated_new,
        attention_moment,
        gated_moment,
        attention_spread,
        gated_spread,
        attention_weights,
        gated_weights,
        attention_averaged,
        gated_averaged,
    )


LANES = 128
HALF = LANES // 2
CLOSE = pl.BlockSpec(memory_space=pltpu.VMEM)
ROOM = pltpu.CompilerParams(vmem_limit_bytes=24 * 2**20)


def here(block):
    return pl.ds(pl.program_id(0) * block.shape[0], block.shape[0])


def by_owner(values, me):
    odd = (me & 1) == 1
    high = (me & 2) == 2
    values = [jnp.where(odd, values[j ^ 1], values[j]) for j in range(4)]
    return [jnp.where(high, values[j ^ 2], values[j]) for j in range(4)]


def fold_sum(block):
    return jnp.sum(block.reshape(-1, 8, LANES), axis=0)


def swap_halves(block):
    return pltpu.roll(block, HALF, 1)


def left_lanes(block):
    return lax.broadcasted_iota(jnp.int32, block.shape, 1) < HALF


def attention_encode_kernel(place, *refs):
    inputs, outputs, sum_ref = refs[:4], refs[4:7], refs[7]

    @pl.when(pl.program_id(0) == 0)
    def _():
        sum_ref[...] = jnp.zeros_like(sum_ref)

    total_squares = sum_ref[...]
    for j in range(4):
        for k in range(inputs[j].shape[0]):
            block = inputs[j][k]
            squared = block * block
            for tile in range(block.shape[1] // LANES):
                total_squares += fold_sum(squared[:, tile * LANES : (tile + 1) * LANES])
            if j:
                outputs[j - 1][k] = encode(block)
    sum_ref[...] = total_squares


def attention_encode(place, gradient, first, count, step):
    mats, rows, cols = gradient.shape
    piece = rows // 4

    def taken(j):
        return pl.BlockSpec((step, piece, cols), lambda i, p: (first // step + i, p[0] ^ j, 0))

    given = pl.BlockSpec((step, piece, cols), lambda i, p: (i, 0, 0))
    return pl.pallas_call(
        attention_encode_kernel,
        grid_spec=pltpu.PrefetchScalarGridSpec(
            num_scalar_prefetch=1,
            grid=(count // step,),
            in_specs=[taken(j) for j in range(4)],
            out_specs=[given] * 3 + [pl.BlockSpec((8, LANES), lambda i, p: (0, 0))],
        ),
        out_shape=[jax.ShapeDtypeStruct((count, piece, cols), jnp.bfloat16)] * 3
        + [jax.ShapeDtypeStruct((8, LANES), jnp.float32)],
        compiler_params=ROOM,
        name="attention_encode",
    )(place, *[gradient] * 4)


def gated_encode_kernel(place, grad_ref, out0, out1, out2, out3, sum_ref, turned):
    me = place[0]

    @pl.when(pl.program_id(0) == 0)
    def _():
        sum_ref[...] = jnp.zeros_like(sum_ref)

    cols, rows = grad_ref.shape[1:]
    block = grad_ref[0]
    squared = block * block
    total_squares = sum_ref[...]
    for tile in range(rows // LANES):
        total_squares += fold_sum(squared[:, tile * LANES : (tile + 1) * LANES])
    sum_ref[...] = total_squares
    code = encode_wide(block)
    turned[:, :cols] = code.T
    piece = rows // 4
    full = cols // LANES
    for j, out in enumerate((out0, out1, out2, out3)):
        start = pl.multiple_of((me ^ j) * piece, piece)
        for tile in range(full):
            lanes = slice(tile * LANES, (tile + 1) * LANES)
            out[0, tile * piece : (tile + 1) * piece, :] = turned[pl.ds(start, piece), lanes].astype(jnp.bfloat16)
        last = turned[pl.ds(start, piece), full * LANES : (full + 1) * LANES]
        upper, lower = last[: piece // 2], last[piece // 2 :]
        out[0, full * piece :, :] = jnp.where(left_lanes(upper), upper, swap_halves(lower)).astype(jnp.bfloat16)


def gated_encode(place, turned_gradient):
    mats, cols, rows = turned_gradient.shape
    packed = rows // 4 * cols // LANES
    given = pl.BlockSpec((1, packed, LANES), lambda i, p: (i, 0, 0))
    return pl.pallas_call(
        gated_encode_kernel,
        grid_spec=pltpu.PrefetchScalarGridSpec(
            num_scalar_prefetch=1,
            grid=(mats,),
            in_specs=[pl.BlockSpec((1, cols, rows), lambda i, p: (i, 0, 0))],
            out_specs=[given] * 4 + [pl.BlockSpec((8, LANES), lambda i, p: (0, 0))],
            scratch_shapes=[pltpu.VMEM((rows, (cols // LANES + 1) * LANES), jnp.float32)],
        ),
        out_shape=[jax.ShapeDtypeStruct((mats, packed, LANES), jnp.bfloat16)] * 4
        + [jax.ShapeDtypeStruct((8, LANES), jnp.float32)],
        compiler_params=ROOM,
        name="gated_encode",
    )(place, turned_gradient)


def update_rows(grads, me, factor, rows, lanes, states, news):
    masters = []
    for a, grad in enumerate(by_owner(grads, me)):
        new = adamw_update(grad, *[ref[0, rows, a, lanes] for ref in states], factor)
        for ref, value in zip(news, new):
            ref[0, rows, a, lanes] = value
        masters.append(new[0])
    return masters


def attention_step_kernel(place, factor_ref, own, in1, in2, in3, *refs):
    me, factor = place[0], factor_ref[0, 0]
    states, news, outs = refs[:3], refs[-7:-4], refs[-4:]
    for start in range(0, own.shape[1], 16):
        rows = pl.ds(start, 16)
        for tile in range(own.shape[2] // LANES):
            lanes = pl.ds(tile * LANES, LANES)
            grads = [own[0, rows, lanes]] + [decode(ref[0, rows, lanes]) for ref in (in1, in2, in3)]
            masters = update_rows(grads, me, factor, rows, lanes, states, news)
            for out, new in zip(outs, by_owner(masters, me)):
                out[0, rows, lanes] = new.astype(jnp.bfloat16)


def attention_step(place, factor, gradient, received, states, before, first, count):
    _, piece, cols = received[0].shape
    state = pl.BlockSpec((1, piece, 4, cols), lambda i, p: (first + i, 0, 0, 0))
    block = pl.BlockSpec((1, piece, cols), lambda i, p: (i, 0, 0))
    taken = pl.BlockSpec((1, piece, cols), lambda i, p: (first + i, 0, 0))
    own = pl.BlockSpec((1, piece, cols), lambda i, p: (first + i, p[0], 0))
    whole = pl.BlockSpec(memory_space=pl.ANY)
    return pl.pallas_call(
        attention_step_kernel,
        grid_spec=pltpu.PrefetchScalarGridSpec(
            num_scalar_prefetch=1,
            grid=(count,),
            in_specs=[pl.BlockSpec(memory_space=pltpu.SMEM), own] + [taken] * 3 + [state] * 3 + [whole] * len(before),
            out_specs=[state] * 3 + [block] * 4,
        ),
        out_shape=[jax.ShapeDtypeStruct(states[0].shape, jnp.float32)] * 3
        + [jax.ShapeDtypeStruct((count, piece, cols), jnp.bfloat16)] * 4,
        input_output_aliases={9 + i: i for i in range(len(before))},
        compiler_params=ROOM,
        name="attention_step",
    )(place, factor, gradient, *received, *states, *before)


def gated_step_kernel(place, factor_ref, in0, in1, in2, in3, *refs):
    me, factor = place[0], factor_ref[0, 0]
    states, news, out, narrow = refs[:3], refs[3:6], refs[6], refs[7]
    ins = (in0, in1, in2, in3)
    piece, cols = states[0].shape[1], states[0].shape[3]
    full, half = cols // LANES, piece // 2
    for tile in range(full):
        lanes = pl.ds(tile * LANES, LANES)
        for start in range(0, piece, 16):
            rows = pl.ds(start, 16)
            grads = [decode(ref[0, pl.ds(tile * piece + start, 16), :]) for ref in ins]
            for a, new in enumerate(update_rows(grads, me, factor, rows, lanes, states, news)):
                narrow[a // 2, pl.ds(a % 2 * piece + start, 16), lanes] = new
    lanes = pl.ds(full * LANES, HALF)
    for start in range(0, half, 16):
        both = [decode(ref[0, pl.ds(full * piece + start, 16), :]) for ref in ins]
        for side in range(2):
            rows = pl.ds(side * half + start, 16)
            grads = [(swap_halves(grad) if side else grad)[:, :HALF] for grad in both]
            for a, new in enumerate(update_rows(grads, me, factor, rows, lanes, states, news)):
                narrow[a // 2, pl.ds(a % 2 * piece + side * half + start, 16), lanes] = new
    middle = cols // 2
    for pair in range(2):
        turned = narrow[pair].T
        top, bottom = turned[:middle], turned[middle:cols]
        left = left_lanes(top)
        out[2 * pair, 0] = jnp.where(left, top, swap_halves(bottom)).astype(jnp.bfloat16)
        out[2 * pair + 1, 0] = jnp.where(left, swap_halves(top), bottom).astype(jnp.bfloat16)


def gated_step(place, factor, received, states):
    count, packed, _ = received[0].shape
    piece, cols = states[0].shape[1], states[0].shape[3]
    state = pl.BlockSpec((1, piece, 4, cols), lambda i, p: (i, 0, 0, 0))
    block = pl.BlockSpec((1, packed, LANES), lambda i, p: (i, 0, 0))
    return pl.pallas_call(
        gated_step_kernel,
        grid_spec=pltpu.PrefetchScalarGridSpec(
            num_scalar_prefetch=1,
            grid=(count,),
            in_specs=[pl.BlockSpec(memory_space=pltpu.SMEM)] + [block] * 4 + [state] * 3,
            out_specs=[state] * 3 + [pl.BlockSpec((4, 1, packed, LANES), lambda i, p: (0, i, 0, 0))],
            scratch_shapes=[pltpu.VMEM((2, LANES, (cols // LANES + 1) * LANES), jnp.float32)],
        ),
        out_shape=[jax.ShapeDtypeStruct(states[0].shape, jnp.float32)] * 3
        + [jax.ShapeDtypeStruct((4, count, packed, LANES), jnp.bfloat16)],
        compiler_params=ROOM,
        name="gated_step",
    )(place, factor, *received, *states)


def attention_place_kernel(place, in0, in1, in2, in3, average, weights, sent, averaged):
    me, section = place[0], place[1]
    piece = in0.shape[1]
    now = here(weights)
    for j, ref in enumerate((in0, in1, in2, in3)):
        weights[:, pl.ds(pl.multiple_of((me ^ j) * piece, piece), piece), :] = ref[now]
    half = 2 * piece
    ours = weights[:, pl.ds(pl.multiple_of(section * half, half), half), :]
    averaged[0] = average_update(average[section, now], ours.astype(jnp.float32))
    sent[...] = weights[:, pl.ds(pl.multiple_of((1 - section) * half, half), half), :]


def attention_place(place, received, average, step):
    mats, piece, cols = received[0].shape
    half = pl.BlockSpec((step, 2 * piece, cols), lambda i, p: (i, 0, 0))
    ours = pl.BlockSpec((1, step, 2 * piece, cols), lambda i, p: (p[1], i, 0, 0))
    return pl.pallas_call(
        attention_place_kernel,
        grid_spec=pltpu.PrefetchScalarGridSpec(
            num_scalar_prefetch=1,
            grid=(mats // step,),
            in_specs=[CLOSE] * 5,
            out_specs=[pl.BlockSpec((step, 4 * piece, cols), lambda i, p: (i, 0, 0)), half, ours],
        ),
        out_shape=[
            jax.ShapeDtypeStruct((mats, 4 * piece, cols), jnp.bfloat16),
            jax.ShapeDtypeStruct((mats, 2 * piece, cols), jnp.bfloat16),
            jax.ShapeDtypeStruct(average.shape, jnp.float32),
        ],
        compiler_params=ROOM,
        name="attention_place",
    )(place, *received, average)


def gated_place_kernel(place, received, average, weights, sent, averaged):
    section, now = place[1], pl.program_id(0)
    blocks = [received[d, now].astype(jnp.float32) for d in range(4)]
    middle = received.shape[2]
    left = left_lanes(blocks[0])
    for tile in range(2):
        lanes = slice(tile * LANES, (tile + 1) * LANES)
        one, two = blocks[2 * tile : 2 * tile + 2]
        weights[0, :middle, lanes] = jnp.where(left, one, swap_halves(two)).astype(jnp.bfloat16)
        weights[0, middle:, lanes] = jnp.where(left, swap_halves(one), two).astype(jnp.bfloat16)
    first, second = weights[0, :, :LANES], weights[0, :, LANES:]

    @pl.when(section == 0)
    def _():
        averaged[0, 0] = average_update(average[0, now], first.astype(jnp.float32))
        sent[0] = second

    @pl.when(section != 0)
    def _():
        averaged[0, 0] = average_update(average[1, now], second.astype(jnp.float32))
        sent[0] = first


def gated_place(place, received, average):
    _, count, packed, _ = received.shape
    half = pl.BlockSpec((1, 2 * packed, LANES), lambda i, p: (i, 0, 0))
    ours = pl.BlockSpec((1, 1, 2 * packed, LANES), lambda i, p: (p[1], i, 0, 0))
    return pl.pallas_call(
        gated_place_kernel,
        grid_spec=pltpu.PrefetchScalarGridSpec(
            num_scalar_prefetch=1,
            grid=(count,),
            in_specs=[CLOSE] * 2,
            out_specs=[pl.BlockSpec((1, 2 * packed, 2 * LANES), lambda i, p: (i, 0, 0)), half, ours],
        ),
        out_shape=[jax.ShapeDtypeStruct((count, 2 * packed, 2 * LANES), jnp.bfloat16)]
        + [jax.ShapeDtypeStruct((count, 2 * packed, LANES), jnp.bfloat16)]
        + [jax.ShapeDtypeStruct(average.shape, jnp.float32)],
        compiler_params=ROOM,
        name="gated_place",
    )(place, received, average)


def average_others_kernel(place, other, average, before, out):
    now = here(out.at[0])
    out[0] = average_update(average[1 - place[1], now], other[now].astype(jnp.float32))


def average_others(place, other, average, before, step):
    count, rows, cols = other.shape
    theirs = pl.BlockSpec((1, step, rows, cols), lambda i, p: (1 - p[1], i, 0, 0))
    return pl.pallas_call(
        average_others_kernel,
        grid_spec=pltpu.PrefetchScalarGridSpec(
            num_scalar_prefetch=1,
            grid=(count // step,),
            in_specs=[CLOSE, CLOSE, pl.BlockSpec(memory_space=pl.ANY)],
            out_specs=theirs,
        ),
        out_shape=jax.ShapeDtypeStruct(average.shape, jnp.float32),
        input_output_aliases={3: 0},
        compiler_params=ROOM,
        name="average_others",
    )(place, other, average, before)


def shards_swap(parts):
    return lax.all_to_all(parts, "shard", split_axis=0, concat_axis=0, tiled=True)


def swap_far_first(values):
    moved = {}
    for j in (3, 2, 1):
        moved[j] = lax.ppermute(values[j - 1], "shard", [(i, i ^ j) for i in range(4)])
    return [moved[j] for j in (1, 2, 3)]


def after(value, done):
    return lax.optimization_barrier((value, done))


def cores(half):
    return lax.ppermute(half, "section", [(0, 1), (1, 0)])


def tuned_shards(
    attention_gradient,
    gated_gradient,
    attention_master,
    gated_master,
    attention_momentum,
    gated_momentum,
    attention_variance,
    gated_variance,
    attention_average,
    gated_average,
):
    place = jnp.stack([lax.axis_index("shard"), lax.axis_index("section")]).astype(jnp.int32)
    mats = attention_gradient.shape[0]
    attention_states = (attention_master, attention_momentum, attention_variance)
    gated_states = (gated_master, gated_momentum, gated_variance)

    *gated_code, gated_squares = gated_encode(place, gated_gradient.swapaxes(1, 2))
    gated_in = gated_code[:1] + swap_far_first(gated_code[1:])
    later_gradient, gated_squares = after(attention_gradient, gated_squares)
    *code, squares = attention_encode(place, later_gradient, 0, mats, 4)
    squares = jnp.sum(gated_squares + squares)
    squares = lax.psum(squares, ("section", "tensor"))
    gated_in, squares = after(gated_in, squares)
    squares = shards_swap(jnp.full((4, 8, LANES), squares))
    code, squares = after(code, squares)
    squares = jnp.sum(squares, axis=0)
    attention_in = swap_far_first(code)
    factor = jnp.minimum(1.0, CLIP_LEVEL * math.sqrt(ENTRIES) / jnp.sqrt(squares[:1, :1]))

    *gated_new, narrow = gated_step(place, factor, gated_in, gated_states)
    narrow, attention_in = after(narrow, attention_in)
    gated_out = shards_swap(narrow)
    *attention_new, own, one, two, three = attention_step(
        place, factor, attention_gradient, attention_in, attention_states, (), 0, mats
    )
    attention_out = [own] + swap_far_first([one, two, three])

    gated_rows = gated_average.swapaxes(2, 3)
    gated_shape = gated_rows.shape
    gated_rows = gated_rows.reshape(2, -1, *gated_shape[2:])
    gated_out, own = after(gated_out, own)
    gated_weights, sent, gated_averaged = gated_place(place, gated_out, gated_rows)
    attention_out, sent = after(attention_out, sent)
    gated_other = cores(sent)

    rows, cols = attention_average.shape[2:]
    attention_rows = attention_average.reshape(2, mats, rows, cols)
    attention_weights, sent, averaged = attention_place(place, attention_out, attention_rows, 2)
    other = cores(sent)
    gated_averaged = average_others(place, gated_other, gated_rows, gated_averaged, 2)
    other, gated_averaged = after(other, gated_averaged)
    averaged = average_others(place, other, attention_rows, averaged, 4)
    gated_averaged = gated_averaged.reshape(gated_shape).swapaxes(2, 3)
    return (
        attention_new[0],
        gated_new[0],
        attention_new[1],
        gated_new[1],
        attention_new[2],
        gated_new[2],
        attention_weights,
        gated_weights.swapaxes(1, 2),
        averaged.reshape(attention_average.shape),
        gated_averaged,
    )


def fits(attention_gradient, gated_gradient, gated_master):
    mats, rows, cols = attention_gradient.shape
    return (
        lax.axis_size("shard") == 4
        and lax.axis_size("section") == 2
        and rows == 2 * LANES
        and cols % LANES == 0
        and mats % 8 == 0
        and gated_gradient.shape[0] % 2 == 0
        and gated_gradient.shape[1] == rows
        and gated_gradient.shape[2] % LANES == HALF
        and gated_master.shape[1:3] == (HALF, 4)
    )


def shards(*arrays):
    if fits(arrays[0], arrays[1], arrays[3]):
        return tuned_shards(*arrays)
    return plain_shards(*arrays)


STATE = P("section", "shard", None, "tensor")
BLOCK = P("section", "shard", "tensor")
ROWS = P(None, "shard", "section", "tensor")


def solution(mesh):
    return jax.shard_map(
        shards,
        mesh=mesh,
        in_specs=(BLOCK,) * 2 + (STATE,) * 6 + (ROWS,) * 2,
        out_specs=(STATE,) * 6 + (BLOCK,) * 2 + (ROWS,) * 2,
        check_vma=False,
    )
```

```python
import math

import jax
import jax.numpy as jnp
from jax import lax
from jax.experimental import pallas as pl
from jax.experimental.pallas import tpu as pltpu
from jax.sharding import PartitionSpec as P

STEP = 20
AVG_COUNT = 3
ENTRIES = 68157440


BETA_FIRST = 0.9
BETA_SECOND = 0.95
ADAM_EPSILON = 1e-08
LEARN_RATE = 0.001
DECAY_RATE = 0.1
CLIP_LEVEL = 0.5

LIFT = 2.0**22


def encode_wide(gradient):
    lifted = gradient * LIFT
    squared = lifted * jnp.abs(lifted)
    return squared * jnp.abs(squared)


def encode(gradient):
    return encode_wide(gradient).astype(jnp.bfloat16)


def decode(code):
    wide = code.astype(jnp.float32)
    root = lax.rsqrt(lax.rsqrt(jnp.abs(wide)))
    return jnp.where(wide < 0, -root, root) * (1.0 / LIFT)


def adamw_update(gradient, master, momentum, variance, factor):
    clipped = gradient * factor
    momentum_new = BETA_FIRST * momentum + (1.0 - BETA_FIRST) * clipped
    variance_new = BETA_SECOND * variance + (1.0 - BETA_SECOND) * clipped * clipped
    first_fix = 1.0 - BETA_FIRST**STEP
    second_fix = 1.0 - BETA_SECOND**STEP
    direction = momentum_new / first_fix / (jnp.sqrt(variance_new / second_fix) + ADAM_EPSILON)
    master_new = master - LEARN_RATE * (direction + DECAY_RATE * master)
    return (master_new, momentum_new, variance_new)


def average_update(average, rows_master):
    return average + (rows_master - average) / (AVG_COUNT + 1.0)


def total(value, axis):
    count = lax.axis_size(axis)
    if count & (count - 1):
        return lax.psum(value, axis)
    step = 1
    while step < count:
        value = value + lax.ppermute(value, axis, [(i, i ^ step) for i in range(count)])
        step *= 2
    return value


def send_gradient(gradient, shard_count):
    mats, rows, cols = gradient.shape
    code = encode(gradient).reshape(mats, shard_count, rows // shard_count, cols)
    return lax.all_to_all(code.transpose(1, 0, 2, 3), "shard", split_axis=0, concat_axis=0, tiled=True)


def send_weights(master):
    narrow = master.astype(jnp.bfloat16).transpose(2, 0, 1, 3)
    blocks = lax.all_to_all(narrow, "shard", split_axis=0, concat_axis=0, tiled=True)
    return blocks.transpose(1, 0, 2, 3).reshape(
        blocks.shape[1], blocks.shape[0] * blocks.shape[2], blocks.shape[3]
    )


def send_halves(weights):
    mats, rows, cols = weights.shape
    count = lax.axis_size("section")
    halves = weights.reshape(mats, count, rows // count, cols)
    halves = lax.all_to_all(halves, "section", split_axis=1, concat_axis=0, tiled=True)
    return halves.astype(jnp.float32)


def plain_shards(
    attention_gradient,
    gated_gradient,
    attention_master,
    gated_master,
    attention_momentum,
    gated_momentum,
    attention_variance,
    gated_variance,
    attention_average,
    gated_average,
):
    shard_count = lax.axis_size("shard")
    gated_piece = send_gradient(gated_gradient, shard_count)
    squares = jnp.sum(attention_gradient * attention_gradient) + jnp.sum(gated_gradient * gated_gradient)
    squares = jnp.full((8, 128), squares)
    for axis in ("section", "tensor"):
        squares = total(squares, axis)
    squares, gated_piece = lax.optimization_barrier((squares, gated_piece))
    squares = total(squares, "shard")
    squares, attention_gradient = lax.optimization_barrier((squares, attention_gradient))
    squares = squares[0, 0]
    attention_piece = send_gradient(attention_gradient, shard_count)
    factor = jnp.minimum(1.0, CLIP_LEVEL * math.sqrt(ENTRIES) / jnp.sqrt(squares))
    gated_new, gated_moment, gated_spread = adamw_update(
        decode(gated_piece).transpose(1, 2, 0, 3), gated_master, gated_momentum, gated_variance, factor
    )
    attention_new, attention_moment, attention_spread = adamw_update(
        decode(attention_piece).transpose(1, 2, 0, 3), attention_master, attention_momentum, attention_variance, factor
    )
    gated_weights = send_weights(gated_new)
    attention_weights = send_weights(attention_new)
    gated_averaged = average_update(gated_average, send_halves(gated_weights))
    attention_averaged = average_update(attention_average, send_halves(attention_weights))
    return (
        attention_new,
        gated_new,
        attention_moment,
        gated_moment,
        attention_spread,
        gated_spread,
        attention_weights,
        gated_weights,
        attention_averaged,
        gated_averaged,
    )


LANES = 128
HALF = LANES // 2
CLOSE = pl.BlockSpec(memory_space=pltpu.VMEM)
ROOM = pltpu.CompilerParams(vmem_limit_bytes=24 * 2**20)


def here(block):
    return pl.ds(pl.program_id(0) * block.shape[0], block.shape[0])


def by_owner(values, me):
    odd = (me & 1) == 1
    high = (me & 2) == 2
    values = [jnp.where(odd, values[j ^ 1], values[j]) for j in range(4)]
    return [jnp.where(high, values[j ^ 2], values[j]) for j in range(4)]


def fold_sum(block):
    return jnp.sum(block.reshape(-1, 8, LANES), axis=0)


def swap_halves(block):
    return pltpu.roll(block, HALF, 1)


def left_lanes(block):
    return lax.broadcasted_iota(jnp.int32, block.shape, 1) < HALF


def attention_encode_kernel(place, *refs):
    inputs, outputs, sum_ref = refs[:4], refs[4:7], refs[7]

    @pl.when(pl.program_id(0) == 0)
    def _():
        sum_ref[...] = jnp.zeros_like(sum_ref)

    total_squares = sum_ref[...]
    for j in range(4):
        for k in range(inputs[j].shape[0]):
            block = inputs[j][k]
            squared = block * block
            for tile in range(block.shape[1] // LANES):
                total_squares += fold_sum(squared[:, tile * LANES : (tile + 1) * LANES])
            if j:
                outputs[j - 1][k] = encode(block)
    sum_ref[...] = total_squares


def attention_encode(place, gradient, first, count, step):
    mats, rows, cols = gradient.shape
    piece = rows // 4

    def taken(j):
        return pl.BlockSpec((step, piece, cols), lambda i, p: (first // step + i, p[0] ^ j, 0))

    given = pl.BlockSpec((step, piece, cols), lambda i, p: (i, 0, 0))
    return pl.pallas_call(
        attention_encode_kernel,
        grid_spec=pltpu.PrefetchScalarGridSpec(
            num_scalar_prefetch=1,
            grid=(count // step,),
            in_specs=[taken(j) for j in range(4)],
            out_specs=[given] * 3 + [pl.BlockSpec((8, LANES), lambda i, p: (0, 0))],
        ),
        out_shape=[jax.ShapeDtypeStruct((count, piece, cols), jnp.bfloat16)] * 3
        + [jax.ShapeDtypeStruct((8, LANES), jnp.float32)],
        compiler_params=ROOM,
        name="attention_encode",
    )(place, *[gradient] * 4)


def gated_encode_kernel(place, grad_ref, out0, out1, out2, out3, sum_ref, turned):
    me = place[0]

    @pl.when(pl.program_id(0) == 0)
    def _():
        sum_ref[...] = jnp.zeros_like(sum_ref)

    cols, rows = grad_ref.shape[1:]
    block = grad_ref[0]
    squared = block * block
    total_squares = sum_ref[...]
    for tile in range(rows // LANES):
        total_squares += fold_sum(squared[:, tile * LANES : (tile + 1) * LANES])
    sum_ref[...] = total_squares
    code = encode_wide(block)
    turned[:, :cols] = code.T
    piece = rows // 4
    full = cols // LANES
    for j, out in enumerate((out0, out1, out2, out3)):
        start = pl.multiple_of((me ^ j) * piece, piece)
        for tile in range(full):
            lanes = slice(tile * LANES, (tile + 1) * LANES)
            out[0, tile * piece : (tile + 1) * piece, :] = turned[pl.ds(start, piece), lanes].astype(jnp.bfloat16)
        last = turned[pl.ds(start, piece), full * LANES : (full + 1) * LANES]
        upper, lower = last[: piece // 2], last[piece // 2 :]
        out[0, full * piece :, :] = jnp.where(left_lanes(upper), upper, swap_halves(lower)).astype(jnp.bfloat16)


def gated_encode(place, turned_gradient):
    mats, cols, rows = turned_gradient.shape
    packed = rows // 4 * cols // LANES
    given = pl.BlockSpec((1, packed, LANES), lambda i, p: (i, 0, 0))
    return pl.pallas_call(
        gated_encode_kernel,
        grid_spec=pltpu.PrefetchScalarGridSpec(
            num_scalar_prefetch=1,
            grid=(mats,),
            in_specs=[pl.BlockSpec((1, cols, rows), lambda i, p: (i, 0, 0))],
            out_specs=[given] * 4 + [pl.BlockSpec((8, LANES), lambda i, p: (0, 0))],
            scratch_shapes=[pltpu.VMEM((rows, (cols // LANES + 1) * LANES), jnp.float32)],
        ),
        out_shape=[jax.ShapeDtypeStruct((mats, packed, LANES), jnp.bfloat16)] * 4
        + [jax.ShapeDtypeStruct((8, LANES), jnp.float32)],
        compiler_params=ROOM,
        name="gated_encode",
    )(place, turned_gradient)


def update_rows(grads, me, factor, rows, lanes, states, news):
    masters = []
    for a, grad in enumerate(by_owner(grads, me)):
        new = adamw_update(grad, *[ref[0, rows, a, lanes] for ref in states], factor)
        for ref, value in zip(news, new):
            ref[0, rows, a, lanes] = value
        masters.append(new[0])
    return masters


def attention_step_kernel(place, factor_ref, own, in1, in2, in3, *refs):
    me, factor = place[0], factor_ref[0, 0]
    states, news, outs = refs[:3], refs[-7:-4], refs[-4:]
    for start in range(0, own.shape[1], 16):
        rows = pl.ds(start, 16)
        for tile in range(own.shape[2] // LANES):
            lanes = pl.ds(tile * LANES, LANES)
            grads = [own[0, rows, lanes]] + [decode(ref[0, rows, lanes]) for ref in (in1, in2, in3)]
            masters = update_rows(grads, me, factor, rows, lanes, states, news)
            for out, new in zip(outs, by_owner(masters, me)):
                out[0, rows, lanes] = new.astype(jnp.bfloat16)


def attention_step(place, factor, gradient, received, states, before, first, count):
    _, piece, cols = received[0].shape
    state = pl.BlockSpec((1, piece, 4, cols), lambda i, p: (first + i, 0, 0, 0))
    block = pl.BlockSpec((1, piece, cols), lambda i, p: (i, 0, 0))
    taken = pl.BlockSpec((1, piece, cols), lambda i, p: (first + i, 0, 0))
    own = pl.BlockSpec((1, piece, cols), lambda i, p: (first + i, p[0], 0))
    whole = pl.BlockSpec(memory_space=pl.ANY)
    return pl.pallas_call(
        attention_step_kernel,
        grid_spec=pltpu.PrefetchScalarGridSpec(
            num_scalar_prefetch=1,
            grid=(count,),
            in_specs=[pl.BlockSpec(memory_space=pltpu.SMEM), own] + [taken] * 3 + [state] * 3 + [whole] * len(before),
            out_specs=[state] * 3 + [block] * 4,
        ),
        out_shape=[jax.ShapeDtypeStruct(states[0].shape, jnp.float32)] * 3
        + [jax.ShapeDtypeStruct((count, piece, cols), jnp.bfloat16)] * 4,
        input_output_aliases={9 + i: i for i in range(len(before))},
        compiler_params=pltpu.CompilerParams(vmem_limit_bytes=58 * 2**20),
        name="attention_step",
    )(place, factor, gradient, *received, *states, *before)


def gated_step_kernel(place, factor_ref, in0, in1, in2, in3, *refs):
    me, factor = place[0], factor_ref[0, 0]
    states, news, out, narrow = refs[:3], refs[3:6], refs[6], refs[7]
    ins = (in0, in1, in2, in3)
    piece, cols = states[0].shape[1], states[0].shape[3]
    full, half = cols // LANES, piece // 2
    for tile in range(full):
        lanes = pl.ds(tile * LANES, LANES)
        for start in range(0, piece, 16):
            rows = pl.ds(start, 16)
            grads = [decode(ref[0, pl.ds(tile * piece + start, 16), :]) for ref in ins]
            for a, new in enumerate(update_rows(grads, me, factor, rows, lanes, states, news)):
                narrow[a // 2, pl.ds(a % 2 * piece + start, 16), lanes] = new
    lanes = pl.ds(full * LANES, HALF)
    for start in range(0, half, 16):
        both = [decode(ref[0, pl.ds(full * piece + start, 16), :]) for ref in ins]
        for side in range(2):
            rows = pl.ds(side * half + start, 16)
            grads = [(swap_halves(grad) if side else grad)[:, :HALF] for grad in both]
            for a, new in enumerate(update_rows(grads, me, factor, rows, lanes, states, news)):
                narrow[a // 2, pl.ds(a % 2 * piece + side * half + start, 16), lanes] = new
    middle = cols // 2
    for pair in range(2):
        turned = narrow[pair].T
        top, bottom = turned[:middle], turned[middle:cols]
        left = left_lanes(top)
        out[2 * pair, 0] = jnp.where(left, top, swap_halves(bottom)).astype(jnp.bfloat16)
        out[2 * pair + 1, 0] = jnp.where(left, swap_halves(top), bottom).astype(jnp.bfloat16)


def gated_step(place, factor, received, states):
    count, packed, _ = received[0].shape
    piece, cols = states[0].shape[1], states[0].shape[3]
    state = pl.BlockSpec((1, piece, 4, cols), lambda i, p: (i, 0, 0, 0))
    block = pl.BlockSpec((1, packed, LANES), lambda i, p: (i, 0, 0))
    return pl.pallas_call(
        gated_step_kernel,
        grid_spec=pltpu.PrefetchScalarGridSpec(
            num_scalar_prefetch=1,
            grid=(count,),
            in_specs=[pl.BlockSpec(memory_space=pltpu.SMEM)] + [block] * 4 + [state] * 3,
            out_specs=[state] * 3 + [pl.BlockSpec((4, 1, packed, LANES), lambda i, p: (0, i, 0, 0))],
            scratch_shapes=[pltpu.VMEM((2, LANES, (cols // LANES + 1) * LANES), jnp.float32)],
        ),
        out_shape=[jax.ShapeDtypeStruct(states[0].shape, jnp.float32)] * 3
        + [jax.ShapeDtypeStruct((4, count, packed, LANES), jnp.bfloat16)],
        compiler_params=pltpu.CompilerParams(vmem_limit_bytes=58 * 2**20),
        name="gated_step",
    )(place, factor, *received, *states)


def attention_place_kernel(place, in0, in1, in2, in3, average, weights, sent, averaged):
    me, section = place[0], place[1]
    piece = in0.shape[1]
    now = here(weights)
    for j, ref in enumerate((in0, in1, in2, in3)):
        weights[:, pl.ds(pl.multiple_of((me ^ j) * piece, piece), piece), :] = ref[now]
    half = 2 * piece
    ours = weights[:, pl.ds(pl.multiple_of(section * half, half), half), :]
    averaged[0] = average_update(average[section, now], ours.astype(jnp.float32))
    sent[...] = weights[:, pl.ds(pl.multiple_of((1 - section) * half, half), half), :]


def attention_place(place, received, average, step):
    mats, piece, cols = received[0].shape
    half = pl.BlockSpec((step, 2 * piece, cols), lambda i, p: (i, 0, 0))
    ours = pl.BlockSpec((1, step, 2 * piece, cols), lambda i, p: (p[1], i, 0, 0))
    return pl.pallas_call(
        attention_place_kernel,
        grid_spec=pltpu.PrefetchScalarGridSpec(
            num_scalar_prefetch=1,
            grid=(mats // step,),
            in_specs=[CLOSE] * 5,
            out_specs=[pl.BlockSpec((step, 4 * piece, cols), lambda i, p: (i, 0, 0)), half, ours],
        ),
        out_shape=[
            jax.ShapeDtypeStruct((mats, 4 * piece, cols), jnp.bfloat16),
            jax.ShapeDtypeStruct((mats, 2 * piece, cols), jnp.bfloat16),
            jax.ShapeDtypeStruct(average.shape, jnp.float32),
        ],
        compiler_params=ROOM,
        name="attention_place",
    )(place, *received, average)


def gated_place_kernel(place, received, average, weights, sent, averaged):
    section, now = place[1], pl.program_id(0)
    blocks = [received[d, now].astype(jnp.float32) for d in range(4)]
    middle = received.shape[2]
    left = left_lanes(blocks[0])
    for tile in range(2):
        lanes = slice(tile * LANES, (tile + 1) * LANES)
        one, two = blocks[2 * tile : 2 * tile + 2]
        weights[0, :middle, lanes] = jnp.where(left, one, swap_halves(two)).astype(jnp.bfloat16)
        weights[0, middle:, lanes] = jnp.where(left, swap_halves(one), two).astype(jnp.bfloat16)
    first, second = weights[0, :, :LANES], weights[0, :, LANES:]

    @pl.when(section == 0)
    def _():
        averaged[0, 0] = average_update(average[0, now], first.astype(jnp.float32))
        sent[0] = second

    @pl.when(section != 0)
    def _():
        averaged[0, 0] = average_update(average[1, now], second.astype(jnp.float32))
        sent[0] = first


def gated_place(place, received, average):
    _, count, packed, _ = received.shape
    half = pl.BlockSpec((1, 2 * packed, LANES), lambda i, p: (i, 0, 0))
    ours = pl.BlockSpec((1, 1, 2 * packed, LANES), lambda i, p: (p[1], i, 0, 0))
    return pl.pallas_call(
        gated_place_kernel,
        grid_spec=pltpu.PrefetchScalarGridSpec(
            num_scalar_prefetch=1,
            grid=(count,),
            in_specs=[CLOSE] * 2,
            out_specs=[pl.BlockSpec((1, 2 * packed, 2 * LANES), lambda i, p: (i, 0, 0)), half, ours],
        ),
        out_shape=[jax.ShapeDtypeStruct((count, 2 * packed, 2 * LANES), jnp.bfloat16)]
        + [jax.ShapeDtypeStruct((count, 2 * packed, LANES), jnp.bfloat16)]
        + [jax.ShapeDtypeStruct(average.shape, jnp.float32)],
        compiler_params=ROOM,
        name="gated_place",
    )(place, received, average)


def average_others_kernel(place, other, average, before, out):
    now = here(out.at[0])
    out[0] = average_update(average[1 - place[1], now], other[now].astype(jnp.float32))


def average_others(place, other, average, before, step):
    count, rows, cols = other.shape
    theirs = pl.BlockSpec((1, step, rows, cols), lambda i, p: (1 - p[1], i, 0, 0))
    return pl.pallas_call(
        average_others_kernel,
        grid_spec=pltpu.PrefetchScalarGridSpec(
            num_scalar_prefetch=1,
            grid=(count // step,),
            in_specs=[CLOSE, CLOSE, pl.BlockSpec(memory_space=pl.ANY)],
            out_specs=theirs,
        ),
        out_shape=jax.ShapeDtypeStruct(average.shape, jnp.float32),
        input_output_aliases={3: 0},
        compiler_params=ROOM,
        name="average_others",
    )(place, other, average, before)


def shards_swap(parts):
    return lax.all_to_all(parts, "shard", split_axis=0, concat_axis=0, tiled=True)


def swap_far_first(values):
    moved = {}
    for j in (3, 2, 1):
        moved[j] = lax.ppermute(values[j - 1], "shard", [(i, i ^ j) for i in range(4)])
    return [moved[j] for j in (1, 2, 3)]


def after(value, done):
    return lax.optimization_barrier((value, done))


def cores(half):
    return lax.ppermute(half, "section", [(0, 1), (1, 0)])


def tuned_shards(
    attention_gradient,
    gated_gradient,
    attention_master,
    gated_master,
    attention_momentum,
    gated_momentum,
    attention_variance,
    gated_variance,
    attention_average,
    gated_average,
):
    place = jnp.stack([lax.axis_index("shard"), lax.axis_index("section")]).astype(jnp.int32)
    mats = attention_gradient.shape[0]
    attention_states = (attention_master, attention_momentum, attention_variance)
    gated_states = (gated_master, gated_momentum, gated_variance)

    *gated_code, gated_squares = gated_encode(place, gated_gradient.swapaxes(1, 2))
    gated_in = gated_code[:1] + swap_far_first(gated_code[1:])
    later_gradient, gated_squares = after(attention_gradient, gated_squares)
    *code, squares = attention_encode(place, later_gradient, 0, mats, 4)
    squares = jnp.sum(gated_squares + squares)
    squares = lax.psum(squares, ("section", "tensor"))
    gated_in, squares = after(gated_in, squares)
    squares = shards_swap(jnp.full((4, 8, LANES), squares))
    code, squares = after(code, squares)
    squares = jnp.sum(squares, axis=0)
    attention_in = swap_far_first(code)
    factor = jnp.minimum(1.0, CLIP_LEVEL * math.sqrt(ENTRIES) / jnp.sqrt(squares[:1, :1]))

    *gated_new, narrow = gated_step(place, factor, gated_in, gated_states)
    narrow, attention_in = after(narrow, attention_in)
    gated_out = shards_swap(narrow)
    *attention_new, own, one, two, three = attention_step(
        place, factor, attention_gradient, attention_in, attention_states, (), 0, mats
    )
    attention_out = [own] + swap_far_first([one, two, three])

    gated_rows = gated_average.swapaxes(2, 3)
    gated_shape = gated_rows.shape
    gated_rows = gated_rows.reshape(2, -1, *gated_shape[2:])
    gated_out, own = after(gated_out, own)
    gated_weights, sent, gated_averaged = gated_place(place, gated_out, gated_rows)
    attention_out, sent = after(attention_out, sent)
    gated_other = cores(sent)

    rows, cols = attention_average.shape[2:]
    attention_rows = attention_average.reshape(2, mats, rows, cols)
    attention_weights, sent, averaged = attention_place(place, attention_out, attention_rows, 8)
    other = cores(sent)
    gated_averaged = average_others(place, gated_other, gated_rows, gated_averaged, 3)
    other, gated_averaged = after(other, gated_averaged)
    averaged = average_others(place, other, attention_rows, averaged, 8)
    gated_averaged = gated_averaged.reshape(gated_shape).swapaxes(2, 3)
    return (
        attention_new[0],
        gated_new[0],
        attention_new[1],
        gated_new[1],
        attention_new[2],
        gated_new[2],
        attention_weights,
        gated_weights.swapaxes(1, 2),
        averaged.reshape(attention_average.shape),
        gated_averaged,
    )


def fits(attention_gradient, gated_gradient, gated_master):
    mats, rows, cols = attention_gradient.shape
    return (
        lax.axis_size("shard") == 4
        and lax.axis_size("section") == 2
        and rows == 2 * LANES
        and cols % LANES == 0
        and mats % 8 == 0
        and gated_gradient.shape[0] % 2 == 0
        and gated_gradient.shape[1] == rows
        and gated_gradient.shape[2] % LANES == HALF
        and gated_master.shape[1:3] == (HALF, 4)
    )


def shards(*arrays):
    if fits(arrays[0], arrays[1], arrays[3]):
        return tuned_shards(*arrays)
    return plain_shards(*arrays)


STATE = P("section", "shard", None, "tensor")
BLOCK = P("section", "shard", "tensor")
ROWS = P(None, "shard", "section", "tensor")


def solution(mesh):
    return jax.shard_map(
        shards,
        mesh=mesh,
        in_specs=(BLOCK,) * 2 + (STATE,) * 6 + (ROWS,) * 2,
        out_specs=(STATE,) * 6 + (BLOCK,) * 2 + (ROWS,) * 2,
        check_vma=False,
    )
```
